256 devices in a mesh: atom: 128 (over z, y, x), wave: 2 (over core).
Axes of the slice: x: 4, y: 4, z: 8, core: 2. Of those that a mesh axis runs over, the one named last changes fastest.
Arguments:
- positions: float32 [3, 32768], P(None, ('atom', 'wave')), may hold values from 0 to 1
- counts: int32 [256], P(('atom', 'wave')), may hold values from 16 to 128, as said below
- feats: bfloat16 [32768, 256], P(('atom', 'wave')), may hold values from -6 to 6
- waves: int32 [3, 8192], P(None, 'wave'), may hold values from -12 to 12
- wave_filter: bfloat16 [8192, 256], P('wave'), may hold values from -5 to 5
- mixing: float32 [256, 256], replicated, may hold values from -0.375 to 0.375
- gain: float32 [256], replicated, may hold values from 0.1 to 1.9
- w_in: bfloat16 [256, 1024], replicated, may hold values from -0.375 to 0.375
- w_out: bfloat16 [1024, 256], replicated, may hold values from -0.1875 to 0.1875
Outputs:
- updated: bfloat16 [32768, 256], P(('atom', 'wave'))
The draws below stay inside these ranges and needn't reach their ends.
Inputs may be any that keep to these rules, and one draw needn't show every extreme that they name: `counts`: each block of 128 slots holds 16 to 128 live atoms at its start; every even-numbered block is full.
All inputs are finite; a program needn't handle non-finite values.
Results may differ from the reference program's by a relative error of at most 0.0055.
Values may be sent and summed in bfloat16 or wider, within the bound.
No kernel may reach another device: no remote copies, remote signals or barrier semaphores. Data moves between devices by JAX's collectives and lax.ppermute only.
A program may use at most 128 MiB of HBM per device.

```python
import math
import jax
import jax.numpy as jnp
from jax import lax

C = 256
HID = 1024
KWAVES = 8192
ATOMS = 32768
BLOCKS = 256


def draw_counts(key, part):
    values = jax.random.randint(jax.random.fold_in(key, 11), (BLOCKS,), 16, 129)
    index = jnp.arange(BLOCKS, dtype=jnp.int32)
    return jnp.where(index % 2 == 0, 128, values).astype(jnp.int32)


def set_ends(drawn, rng, least, top_value):
    shape = drawn.shape
    place = [jax.random.randint(jax.random.fold_in(rng, axis), (), 0, shape[axis]) for axis in range(len(shape))]
    drawn = drawn.at[tuple(place)].set(least)
    longest = shape.index(max(shape))
    place[longest] = (place[longest] + 1) % shape[longest]
    return drawn.at[tuple(place)].set(top_value)


def levels(rng, shape, split, low, high):
    level, own = 1.0, jax.random.fold_in(rng, 6)
    for axis_at, parts in split:
        steps = jnp.exp(jax.random.uniform(jax.random.fold_in(own, axis_at), (parts,), jnp.float32, low / len(split), high / len(split)))
        level = level * jnp.repeat(steps, shape[axis_at] // parts).reshape([-1 if axis == axis_at else 1 for axis in range(len(shape))])
    return level


def normal_values(stream_key, extent, deviation, limit, split=(), kind=jnp.bfloat16):
    level = levels(stream_key, extent, split, -0.22, 0.18) if split else 1.0
    drawn = jax.random.normal(stream_key, extent, jnp.float32) * deviation * level
    return jnp.minimum(jnp.maximum(drawn, -limit), limit).astype(kind)


def setup_inputs(seed: int = 0) -> dict:
    seeds = jax.random.split(jax.random.key(seed), 10)
    positions = jnp.clip(1.0 * jax.random.uniform(seeds[0], (3, ATOMS), jnp.float32) ** levels(seeds[0], (3, ATOMS), ((1, 256),), -0.2, 0.2), 0.0, 1.0)
    counts = draw_counts(jax.random.fold_in(seeds[9], 71), 0)
    feats = normal_values(seeds[2], (ATOMS, C), 1.0, 6.0, ((0, 256),))
    waves = set_ends(jax.random.randint(seeds[3], (3, KWAVES), -12, 13), jax.random.fold_in(seeds[3], 1), -12, 12).astype(jnp.int32)
    wave_filter = normal_values(seeds[4], (KWAVES, C), 1.0, 5.0, ((0, 2),))
    mixing = normal_values(seeds[5], (C, C), C ** -0.5, 0.375, (), jnp.float32)
    gain = jnp.clip(1.0 + 0.18 * jax.random.normal(seeds[6], (C,), jnp.float32), 0.1, 1.9)
    w_in = normal_values(seeds[7], (C, HID), C ** -0.5, 0.375)
    w_out = normal_values(seeds[8], (HID, C), HID ** -0.5, 0.1875)
    return dict(positions=positions, counts=counts, feats=feats, waves=waves, wave_filter=wave_filter, mixing=mixing, gain=gain, w_in=w_in, w_out=w_out)


two_pi = 2.0 * math.pi

def phases(coords, wave_f):
    return (coords[0][:, None] * wave_f[0][None, :] + coords[1][:, None] * wave_f[1][None, :] + coords[2][:, None] * wave_f[2][None, :]) * two_pi

def reference(positions, counts, feats, waves, wave_filter, mixing, gain, w_in, w_out):
    slot = lax.broadcasted_iota(jnp.int32, (BLOCKS, 128), 1)
    live = (slot < counts[:, None]).reshape(ATOMS)
    masked = feats * live[:, None].astype(jnp.bfloat16)
    wave_f = waves.astype(jnp.float32)
    size = 512 if ATOMS % 512 == 0 else 128
    steps_n = ATOMS // size

    def forward(carry, index):
        start = (index * size).astype(jnp.int32)
        coords = lax.dynamic_slice_in_dim(positions, start, size, 1)
        rows_h = lax.dynamic_slice_in_dim(masked, start, size, 0)
        angle = phases(coords, wave_f)
        cosine = jnp.cos(angle).astype(jnp.bfloat16)
        sine = jnp.sin(angle).astype(jnp.bfloat16)
        real_add = jnp.dot(cosine.T, rows_h, preferred_element_type=jnp.float32)
        imag_add = jnp.dot(sine.T, rows_h, preferred_element_type=jnp.float32)
        return ((carry[0] + real_add, carry[1] + imag_add), None)
    zero = jnp.zeros((KWAVES, C), jnp.float32)
    (real_sum, imag_sum), _ = lax.scan(forward, (zero, zero), jnp.arange(steps_n, dtype=jnp.int32))
    scale = 1.0 / math.sqrt(ATOMS)
    filt = wave_filter.astype(jnp.float32)
    filtered_real = jnp.dot(real_sum * scale * filt, mixing, precision=lax.Precision.HIGHEST).astype(jnp.bfloat16)
    filtered_imag = jnp.dot(imag_sum * scale * filt, mixing, precision=lax.Precision.HIGHEST).astype(jnp.bfloat16)
    inv_k = 1.0 / math.sqrt(KWAVES)

    def inverse(index):
        start = (index * size).astype(jnp.int32)
        coords = lax.dynamic_slice_in_dim(positions, start, size, 1)
        angle = phases(coords, wave_f)
        cosine = jnp.cos(angle).astype(jnp.bfloat16)
        sine = jnp.sin(angle).astype(jnp.bfloat16)
        field = jnp.dot(cosine, filtered_real, preferred_element_type=jnp.float32) + jnp.dot(sine, filtered_imag, preferred_element_type=jnp.float32)
        return field * inv_k
    update = lax.map(inverse, jnp.arange(steps_n, dtype=jnp.int32)).reshape(ATOMS, C)
    state = feats.astype(jnp.float32) + update
    meansq = lax.optimization_barrier(jnp.mean(state * state, axis=1, keepdims=True))
    normed = (state * lax.rsqrt(meansq + 1e-06) * gain[None, :]).astype(jnp.bfloat16)
    hidden = jax.nn.silu(jnp.dot(normed, w_in, preferred_element_type=jnp.float32)).astype(jnp.bfloat16)
    result = state + jnp.dot(hidden, w_out, preferred_element_type=jnp.float32)
    return jnp.where(live[:, None], result, 0.0).astype(jnp.bfloat16)
```

```python
import math

import jax
import jax.numpy as jnp
from jax import lax
from jax.experimental import pallas as pl
from jax.experimental.pallas import tpu as pltpu
from jax.sharding import Mesh
from jax.sharding import PartitionSpec as P

bf16 = jnp.bfloat16
f32 = jnp.float32

NZ, NY, NX, NC = 8, 4, 4, 2
NYX = NY * NX
HALF = NZ // 2


ROOT2 = math.sqrt(2.0)
SIN_C = (
    3.1415926520468305,
    -5.167710734303894,
    2.550084223872135,
    -0.5983094608569061,
    0.07765872505863924,
)
COS_C = (
    0.9999999946405678,
    -4.934795092504032,
    4.058434665884265,
    -1.3319399977127386,
    0.21969398917152252,
)
MAGIC = 1.5 * 2.0**23


def poly(coefs, w):
    acc = coefs[-1] * ROOT2
    for c in coefs[-2::-1]:
        acc = acc * w + c * ROOT2
    return acc


def cos_sin(turns):
    u = turns - ((turns + MAGIC) - MAGIC)
    w = u * u
    s = u * poly(SIN_C, w)
    c = poly(COS_C, w)
    return 1.0 - s * s, s * c


def pack_kernel(count_ref, pos_ref, feats_ref, out_ref):
    rows = feats_ref.shape[0]
    slot = lax.broadcasted_iota(jnp.int32, feats_ref.shape, 0)
    live = slot < count_ref[0]
    feats = feats_ref[...].astype(f32)
    out_ref[0:rows, :] = jnp.where(live, feats, 0.0).astype(bf16)
    pos = pos_ref[...]
    hi = pos.astype(bf16).astype(f32)
    rest = pos - hi
    mid = rest.astype(bf16).astype(f32)
    low = rest - mid
    n = pos.shape[1]
    tail = jnp.concatenate([hi, mid, low, jnp.zeros((7, n), f32)], axis=0)
    out_ref[rows : rows + 16, :] = jnp.concatenate(
        [tail, jnp.zeros((16, feats.shape[1] - n), f32)], axis=1
    ).astype(bf16)


def pack(counts, positions, feats):
    rows, width = feats.shape
    return pl.pallas_call(
        pack_kernel,
        out_shape=jax.ShapeDtypeStruct((rows + 16, width), bf16),
        in_specs=[
            pl.BlockSpec(memory_space=pltpu.SMEM),
            pl.BlockSpec(memory_space=pltpu.VMEM),
            pl.BlockSpec(memory_space=pltpu.VMEM),
        ],
        out_specs=pl.BlockSpec(memory_space=pltpu.VMEM),
        name="pack_atoms",
    )(counts, positions, feats)


OWN = 32
STEP = 256


def factors(waves9, blocks, dtype):
    rows = waves9.shape[0]
    width = blocks[0].shape[1]
    n = blocks[0].shape[0] - 16
    nb = len(blocks)
    atoms = n * nb
    piece = 512
    groups = STEP // OWN

    def kernel(*refs):
        waves_ref = refs[0]
        block_refs = refs[1 : 1 + nb]
        out_ref, tile_ref, feats, coords, turns = refs[1 + nb :]

        @pl.when(pl.program_id(0) == 0)
        def _():
            for j, block in enumerate(block_refs):
                feats[j * n : (j + 1) * n, :] = block[0:n, :]
                coords[:, j * n : (j + 1) * n] = block[n : n + 16, 0:n]

        turns[...] = jnp.dot(waves_ref[...], coords[...], preferred_element_type=f32)

        def step(i, carry):
            for h in range(0, OWN, 16):
                at = pl.ds(pl.multiple_of(i * OWN + h, 16), 16)
                to_cos = pl.ds(pl.multiple_of(i * 2 * OWN + h, 16), 16)
                to_sin = pl.ds(pl.multiple_of(i * 2 * OWN + OWN + h, 16), 16)
                for q in range(0, atoms, piece):
                    c, s = cos_sin(turns[at, q : q + piece])
                    tile_ref[to_cos, q : q + piece] = c.astype(bf16)
                    tile_ref[to_sin, q : q + piece] = s.astype(bf16)
            return carry

        lax.fori_loop(0, groups, step, 0)
        summed = jnp.dot(tile_ref[...], feats[...], preferred_element_type=f32)
        out_ref[...] = summed.astype(dtype).reshape(groups, 2, OWN, width)

    return pl.pallas_call(
        kernel,
        grid=(rows // STEP,),
        out_shape=(
            jax.ShapeDtypeStruct((rows // OWN, 2, OWN, width), dtype),
            jax.ShapeDtypeStruct((2 * rows, atoms), bf16),
        ),
        in_specs=[pl.BlockSpec((STEP, 16), lambda i: (i, 0))]
        + [pl.BlockSpec(b.shape, lambda i: (0, 0)) for b in blocks],
        out_specs=(
            pl.BlockSpec((groups, 2, OWN, width), lambda i: (i, 0, 0, 0)),
            pl.BlockSpec((2 * STEP, atoms), lambda i: (i, 0)),
        ),
        scratch_shapes=[
            pltpu.VMEM((atoms, width), bf16),
            pltpu.VMEM((16, atoms), bf16),
            pltpu.VMEM((STEP, atoms), f32),
        ],
        cost_estimate=pl.CostEstimate(
            flops=4 * rows * atoms * width, transcendentals=0, bytes_accessed=4 * rows * atoms
        ),
        name="structure_factors",
    )(waves9, *blocks)


def filter_kernel(arrived_ref, filt_ref, mix_ref, out_ref, *, scale):
    n = arrived_ref.shape[0]
    total = arrived_ref[0].astype(f32)
    for j in range(1, n):
        total = total + arrived_ref[j].astype(f32)
    filt = filt_ref[...].astype(f32)
    both = jnp.concatenate([total[0] * scale * filt, total[1] * scale * filt], axis=0)
    mixed = jnp.dot(
        both, mix_ref[...], precision=lax.Precision.HIGHEST, preferred_element_type=f32
    ).astype(bf16)
    rows = filt.shape[0]
    for j in range(n):
        out_ref[j, 0] = mixed[:rows]
        out_ref[j, 1] = mixed[rows:]


def filter_mix(arrived, filt, mixing, scale):
    vmem = pl.BlockSpec(memory_space=pltpu.VMEM)
    return pl.pallas_call(
        lambda *refs: filter_kernel(*refs, scale=scale),
        out_shape=jax.ShapeDtypeStruct(arrived.shape, bf16),
        in_specs=[vmem] * 3,
        out_specs=vmem,
        name="filter_mix",
    )(arrived, filt, mixing)


def fields(tiles, halves, first, dtypes, after=()):
    owners, two, own, width = halves[0].shape
    half = owners * two * own
    n = 128
    count = len(dtypes)

    def kernel(*refs):
        tile_refs, half_refs = refs[:2], refs[2:4]
        out_refs = refs[4 + len(after) :]
        field = None
        for f, tile in zip(half_refs, tile_refs):
            lhs = f[...].reshape(half, width).T
            part = jnp.dot(
                lhs, tile[:, first * n : (first + count) * n], preferred_element_type=f32
            )
            field = part if field is None else field + part
        for j, out in enumerate(out_refs):
            out[...] = field[:, j * n : (j + 1) * n].astype(out.dtype)

    vmem = pl.BlockSpec(memory_space=pltpu.VMEM)
    return pl.pallas_call(
        kernel,
        out_shape=tuple(jax.ShapeDtypeStruct((width, n), d) for d in dtypes),
        in_specs=[vmem] * 4 + [pl.BlockSpec(memory_space=pl.ANY)] * len(after),
        out_specs=(vmem,) * count,
        cost_estimate=pl.CostEstimate(
            flops=4 * half * width * n * count,
            transcendentals=0,
            bytes_accessed=4 * half * n * count,
        ),
        name="wave_fields",
    )(*tiles, *halves, *after)


def update_kernel(count_ref, *refs, scale):
    part_refs = refs[:-5]
    feats_ref, gain_ref, win_ref, wout_ref, out_ref = refs[-5:]
    total = part_refs[0][...].astype(f32)
    for part in part_refs[1:]:
        total = total + part[...].astype(f32)
    state = feats_ref[...].astype(f32) + (total * scale).T
    meansq = jnp.mean(state * state, axis=1, keepdims=True)
    normed = (state * lax.rsqrt(meansq + 1e-06) * gain_ref[...]).astype(bf16)
    v = jnp.dot(normed, win_ref[...], preferred_element_type=f32)
    hidden = (v / (1.0 + jnp.exp(-v))).astype(bf16)
    result = state + jnp.dot(hidden, wout_ref[...], preferred_element_type=f32)
    slot = lax.broadcasted_iota(jnp.int32, result.shape, 0)
    out_ref[...] = jnp.where(slot < count_ref[0], result, 0.0).astype(bf16)


def update(counts, parts, feats, gain, w_in, w_out, scale):
    vmem = pl.BlockSpec(memory_space=pltpu.VMEM)
    return pl.pallas_call(
        lambda *refs: update_kernel(*refs, scale=scale),
        out_shape=jax.ShapeDtypeStruct(feats.shape, bf16),
        in_specs=[pl.BlockSpec(memory_space=pltpu.SMEM)] + [vmem] * (len(parts) + 4),
        out_specs=vmem,
        name="update_atoms",
    )(counts, *parts, feats, gain[None, :], w_in, w_out)


def body(positions, counts, feats, waves, wave_filter, mixing, gain, w_in, w_out):
    kw = waves.shape[1]
    share = kw // NZ
    own_waves = share // NYX
    atoms_all = feats.shape[0] * NZ * NYX * NC
    kwaves_all = kw * NC
    z = lax.axis_index("z")
    yx = lax.axis_index("y") * NX + lax.axis_index("x")
    order = [HALF] + [d for s in range(HALF - 1, 0, -1) for d in (s, -s)] + [0]
    swap = [(0, 1), (1, 0)]

    def partner(v):
        return lax.ppermute(v, "core", swap)

    def shift(v, d):
        return lax.ppermute(v, "z", [(i, (i + d) % NZ) for i in range(NZ)]) if d else v

    def exchange(v):
        return lax.all_to_all(v, ("y", "x"), 0, 0, tiled=True)

    block = pack(counts, positions, feats)
    mine = lax.dynamic_slice_in_dim(waves, z * share, share, 1).astype(bf16)
    other = partner(mine)
    both = jnp.concatenate([other, mine], axis=1)
    waves9 = jnp.pad(jnp.concatenate([both] * 3, axis=0), ((0, 7), (0, 0))).T

    blocks = [shift(block, -d) for d in order]
    sent, tile_other = factors(waves9[:share], blocks, bf16)
    arrived = partner(sent)
    kept, tile_mine = factors(waves9[share:], blocks, f32)
    summed = exchange((kept + arrived.astype(f32)).astype(bf16))
    filt = lax.dynamic_slice_in_dim(wave_filter, z * share + yx * own_waves, own_waves, 0)
    spread = filter_mix(summed, filt, mixing, 1.0 / math.sqrt(atoms_all))
    filtered = exchange(spread)
    halves = (partner(filtered), filtered)

    tiles = (tile_other, tile_mine)
    far = fields(tiles, halves, 0, [bf16] * 3)
    parts = far + fields(tiles, halves, 3, [bf16] * (NZ - 4) + [f32], far[:1])
    parts = [shift(part, d) for part, d in zip(parts, order)]
    return update(counts, parts, feats, gain, w_in, w_out, 1.0 / math.sqrt(kwaves_all))


def solution(mesh):
    fine = Mesh(mesh.devices.reshape(NZ, NY, NX, NC), ("z", "y", "x", "core"))
    every = ("z", "y", "x", "core")
    return jax.shard_map(
        body,
        mesh=fine,
        in_specs=(
            P(None, every),
            P(every),
            P(every, None),
            P(None, "core"),
            P("core", None),
            P(),
            P(),
            P(),
            P(),
        ),
        out_specs=P(every, None),
        check_vma=False,
    )
```

```python
import math

import jax
import jax.numpy as jnp
from jax import lax
from jax.experimental import pallas as pl
from jax.experimental.pallas import tpu as pltpu
from jax.sharding import Mesh
from jax.sharding import PartitionSpec as P

bf16 = jnp.bfloat16
f32 = jnp.float32

NZ, NY, NX, NC = 8, 4, 4, 2
NYX = NY * NX
HALF = NZ // 2


ROOT2 = math.sqrt(2.0)
SIN_C = (
    3.1415926520468305,
    -5.167710734303894,
    2.550084223872135,
    -0.5983094608569061,
    0.07765872505863924,
)
COS_C = (
    0.9999999946405678,
    -4.934795092504032,
    4.058434665884265,
    -1.3319399977127386,
    0.21969398917152252,
)
MAGIC = 1.5 * 2.0**23


def poly(coefs, w):
    acc = coefs[-1] * ROOT2
    for c in coefs[-2::-1]:
        acc = acc * w + c * ROOT2
    return acc


def cos_sin(turns):
    u = turns - ((turns + MAGIC) - MAGIC)
    w = u * u
    s = u * poly(SIN_C, w)
    c = poly(COS_C, w)
    return 1.0 - s * s, s * c


VMEM = pl.BlockSpec(memory_space=pltpu.VMEM)
SMALL = pltpu.CompilerParams(vmem_limit_bytes=16 << 20)


def on_chip(*values):
    return [pltpu.with_memory_space_constraint(v, pltpu.VMEM) for v in values]


def in_hbm(*values):
    return [pltpu.with_memory_space_constraint(v, pltpu.HBM) for v in values]


def pack_kernel(count_ref, _z, _slot, pos_ref, feats_ref, waves_ref, filt_ref, out_ref, waves_out, filt_out):
    rows = feats_ref.shape[0]
    waves = waves_ref[...].astype(f32)
    waves_out[...] = jnp.concatenate(
        [waves, waves, waves, jnp.zeros((7, waves.shape[1]), f32)], axis=0
    ).astype(bf16)
    filt_out[...] = filt_ref[...]
    slot = lax.broadcasted_iota(jnp.int32, feats_ref.shape, 0)
    live = slot < count_ref[0]
    feats = feats_ref[...].astype(f32)
    out_ref[0:rows, :] = jnp.where(live, feats, 0.0).astype(bf16)
    pos = pos_ref[...]
    hi = pos.astype(bf16).astype(f32)
    rest = pos - hi
    mid = rest.astype(bf16).astype(f32)
    low = rest - mid
    n = pos.shape[1]
    tail = jnp.concatenate([hi, mid, low, jnp.zeros((7, n), f32)], axis=0)
    out_ref[rows : rows + 16, :] = jnp.concatenate(
        [tail, jnp.zeros((16, feats.shape[1] - n), f32)], axis=1
    ).astype(bf16)


def pack(counts, z, slot, positions, feats, waves, wave_filter, share, own):
    rows, width = feats.shape

    def whole(v):
        return pl.BlockSpec(v.shape, lambda i, c, z, s: (0, 0))

    return pl.pallas_call(
        pack_kernel,
        grid_spec=pltpu.PrefetchScalarGridSpec(
            num_scalar_prefetch=3,
            grid=(1,),
            in_specs=[
                whole(positions),
                whole(feats),
                pl.BlockSpec((3, share), lambda i, c, z, s: (0, z[0])),
                pl.BlockSpec((own, width), lambda i, c, z, s: (s[0], 0)),
            ],
            out_specs=(
                pl.BlockSpec((rows + 16, width), lambda i, c, z, s: (0, 0)),
                pl.BlockSpec((16, share), lambda i, c, z, s: (0, 0)),
                pl.BlockSpec((own, width), lambda i, c, z, s: (0, 0)),
            ),
        ),
        out_shape=(
            jax.ShapeDtypeStruct((rows + 16, width), bf16),
            jax.ShapeDtypeStruct((16, share), bf16),
            jax.ShapeDtypeStruct((own, width), bf16),
        ),
        compiler_params=SMALL,
        name="pack_atoms",
    )(counts, z[None], slot[None], *in_hbm(positions, feats, waves, wave_filter))


OWN = 32


def factors(waves9, blocks, dtype):
    rows = waves9.shape[1]
    width = blocks[0].shape[1]
    n = min(b.shape[0] for b in blocks) - 16
    nb = len(blocks)
    held = [b.shape[0] // (n + 16) for b in blocks]
    atoms = n * sum(held)
    piece = 512
    groups = rows // OWN

    def kernel(*refs):
        waves_ref = refs[0]
        block_refs = refs[1 : 1 + nb]
        out_ref, tile_ref, feats, coords, turns = refs[1 + nb :]
        j = 0
        for block, count in zip(block_refs, held):
            for k in range(count):
                at = k * (n + 16)
                feats[j * n : (j + 1) * n, :] = block[at : at + n, :]
                coords[:, j * n : (j + 1) * n] = block[at + n : at + n + 16, 0:n]
                j += 1
        turns[...] = jnp.dot(
            waves_ref[...].astype(f32).T.astype(bf16), coords[...], preferred_element_type=f32
        )

        def step(i, carry):
            for h in range(0, OWN, 16):
                at = pl.ds(pl.multiple_of(i * OWN + h, 16), 16)
                to_cos = pl.ds(pl.multiple_of(i * 2 * OWN + h, 16), 16)
                to_sin = pl.ds(pl.multiple_of(i * 2 * OWN + OWN + h, 16), 16)
                for q in range(0, atoms, piece):
                    c, s = cos_sin(turns[at, q : q + piece])
                    tile_ref[to_cos, q : q + piece] = c.astype(bf16)
                    tile_ref[to_sin, q : q + piece] = s.astype(bf16)
            return carry

        lax.fori_loop(0, groups, step, 0)
        summed = jnp.dot(tile_ref[...], feats[...], preferred_element_type=f32)
        out_ref[...] = summed.astype(dtype).reshape(groups, 2, OWN, width)

    return pl.pallas_call(
        kernel,
        out_shape=(
            pltpu.VMEM((groups, 2, OWN, width), dtype),
            pltpu.VMEM((2 * rows, atoms), bf16),
        ),
        in_specs=[VMEM] * (1 + nb),
        out_specs=(VMEM, VMEM),
        scratch_shapes=[
            pltpu.VMEM((atoms, width), bf16),
            pltpu.VMEM((16, atoms), bf16),
            pltpu.VMEM((rows, atoms), f32),
        ],
        cost_estimate=pl.CostEstimate(
            flops=4 * rows * atoms * width, transcendentals=0, bytes_accessed=4 * rows * atoms
        ),
        compiler_params=SMALL,
        name="structure_factors",
    )(*on_chip(waves9, *blocks))


def filter_kernel(arrived_ref, filt_ref, mix_ref, out_ref, *, scale):
    n = arrived_ref.shape[0]
    total = arrived_ref[0].astype(f32)
    for j in range(1, n):
        total = total + arrived_ref[j].astype(f32)
    filt = filt_ref[...].astype(f32)
    both = jnp.concatenate([total[0] * scale * filt, total[1] * scale * filt], axis=0)
    mixed = jnp.dot(
        both, mix_ref[...], precision=lax.Precision.HIGHEST, preferred_element_type=f32
    ).astype(bf16)
    rows = filt.shape[0]
    for j in range(n):
        out_ref[j, 0] = mixed[:rows]
        out_ref[j, 1] = mixed[rows:]


def filter_mix(arrived, filt, mixing, scale):
    return pl.pallas_call(
        lambda *refs: filter_kernel(*refs, scale=scale),
        out_shape=pltpu.VMEM(arrived.shape, bf16),
        in_specs=[VMEM] * 3,
        out_specs=VMEM,
        compiler_params=SMALL,
        name="filter_mix",
    )(*on_chip(arrived, filt, mixing))


def fields(tiles, halves, first, outs, after=()):
    owners, two, own, width = halves[0].shape
    half = owners * two * own
    n = 128
    count = sum(blocks for blocks, _ in outs)

    def kernel(*refs):
        tile_refs, half_refs = refs[:2], refs[2:4]
        out_refs = refs[4 + len(after) :]
        field = None
        for f, tile in zip(half_refs, tile_refs):
            lhs = f[...].reshape(half, width).T
            part = jnp.dot(
                lhs, tile[:, first * n : (first + count) * n], preferred_element_type=f32
            )
            field = part if field is None else field + part
        j = 0
        for out in out_refs:
            for k in range(out.shape[0]):
                out[k] = field[:, j * n : (j + 1) * n].astype(out.dtype)
                j += 1

    return pl.pallas_call(
        kernel,
        out_shape=tuple(pltpu.VMEM((blocks, width, n), d) for blocks, d in outs),
        in_specs=[VMEM] * 4 + [pl.BlockSpec(memory_space=pl.ANY)] * len(after),
        out_specs=(VMEM,) * len(outs),
        cost_estimate=pl.CostEstimate(
            flops=4 * half * width * n * count,
            transcendentals=0,
            bytes_accessed=4 * half * n * count,
        ),
        compiler_params=SMALL,
        name="wave_fields",
    )(*on_chip(*tiles, *halves), *after)


def update_kernel(count_ref, *refs, scale):
    part_refs = refs[:-5]
    feats_ref, gain_ref, win_ref, wout_ref, out_ref = refs[-5:]
    total = part_refs[0][0].astype(f32)
    for part in part_refs[1:]:
        total = total + part[0].astype(f32)
    state = feats_ref[...].astype(f32) + (total * scale).T
    meansq = jnp.mean(state * state, axis=1, keepdims=True)
    normed = (state * lax.rsqrt(meansq + 1e-06) * gain_ref[...]).astype(bf16)
    v = jnp.dot(normed, win_ref[...], preferred_element_type=f32)
    hidden = (v / (1.0 + jnp.exp(-v))).astype(bf16)
    result = state + jnp.dot(hidden, wout_ref[...], preferred_element_type=f32)
    slot = lax.broadcasted_iota(jnp.int32, result.shape, 0)
    out_ref[...] = jnp.where(slot < count_ref[0], result, 0.0).astype(bf16)


def update(counts, parts, feats, gain, w_in, w_out, scale):
    return pl.pallas_call(
        lambda *refs: update_kernel(*refs, scale=scale),
        out_shape=jax.ShapeDtypeStruct(feats.shape, bf16),
        in_specs=[pl.BlockSpec(memory_space=pltpu.SMEM)] + [VMEM] * (len(parts) + 4),
        out_specs=VMEM,
        compiler_params=SMALL,
        name="update_atoms",
    )(counts, *on_chip(*parts, feats, gain[None, :], w_in, w_out))


def body(positions, counts, feats, waves, wave_filter, mixing, gain, w_in, w_out):
    kw = waves.shape[1]
    share = kw // NZ
    own_waves = share // NYX
    atoms_all = feats.shape[0] * NZ * NYX * NC
    kwaves_all = kw * NC
    z = lax.axis_index("z")
    yx = lax.axis_index("y") * NX + lax.axis_index("x")
    swap = [(0, 1), (1, 0)]

    def partner(v):
        return lax.ppermute(v, "core", swap)

    def shift(v, d):
        return lax.ppermute(v, "z", [(i, (i + d) % NZ) for i in range(NZ)]) if d else v

    def exchange(v):
        return lax.all_to_all(v, ("y", "x"), 0, 0, tiled=True)

    block, mine, filt = pack(
        counts, z, z * NYX + yx, positions, feats, waves, wave_filter, share, own_waves
    )
    other = partner(mine)
    opposite = shift(block, HALF)
    ahead = shift(block, -2)
    behind = shift(block, 2)
    pair = jnp.concatenate([block, opposite], axis=0)
    blocks = [shift(pair, 1), shift(pair, -1), ahead, behind, opposite, block]
    sent, tile_other = factors(other, blocks, bf16)
    arrived = partner(sent)
    kept, tile_mine = factors(mine, blocks, f32)
    summed = exchange((kept + arrived.astype(f32)).astype(bf16))
    spread = filter_mix(summed, filt, mixing, 1.0 / math.sqrt(atoms_all))
    filtered = exchange(spread)
    halves = (partner(filtered), filtered)

    tiles = (tile_other, tile_mine)
    to_behind, to_ahead = fields(tiles, halves, 0, [(2, bf16), (2, bf16)])
    two_ahead, two_behind, far, own = fields(
        tiles, halves, 4, [(1, bf16), (1, bf16), (1, f32), (1, f32)], (to_ahead,)
    )
    from_ahead = shift(to_behind, -1)
    from_behind = shift(to_ahead, 1)
    passed = far + (from_ahead[1:].astype(f32) + from_behind[1:].astype(f32))
    parts = [own, from_ahead, from_behind, shift(two_ahead, 2), shift(two_behind, -2)]
    parts.append(shift(passed.astype(bf16), HALF))
    return update(counts, parts, feats, gain, w_in, w_out, 1.0 / math.sqrt(kwaves_all))


def solution(mesh):
    fine = Mesh(mesh.devices.reshape(NZ, NY, NX, NC), ("z", "y", "x", "core"))
    every = ("z", "y", "x", "core")
    return jax.shard_map(
        body,
        mesh=fine,
        in_specs=(
            P(None, every),
            P(every),
            P(every, None),
            P(None, "core"),
            P("core", None),
            P(),
            P(),
            P(),
            P(),
        ),
        out_specs=P(every, None),
        check_vma=False,
    )
```

```python
import math

import jax
import jax.numpy as jnp
from jax import lax
from jax.experimental import pallas as pl
from jax.experimental.pallas import tpu as pltpu
from jax.sharding import Mesh
from jax.sharding import PartitionSpec as P

bf16 = jnp.bfloat16
f32 = jnp.float32

NZ, NY, NX, NC = 8, 4, 4, 2
NYX = NY * NX
HALF = NZ // 2


ROOT2 = math.sqrt(2.0)
SIN_C = (
    3.1415926520468305,
    -5.167710734303894,
    2.550084223872135,
    -0.5983094608569061,
    0.07765872505863924,
)
COS_C = (
    0.9999999946405678,
    -4.934795092504032,
    4.058434665884265,
    -1.3319399977127386,
    0.21969398917152252,
)
MAGIC = 1.5 * 2.0**23


def poly(coefs, w):
    acc = coefs[-1] * ROOT2
    for c in coefs[-2::-1]:
        acc = acc * w + c * ROOT2
    return acc


def cos_sin(turns):
    u = turns - ((turns + MAGIC) - MAGIC)
    w = u * u
    s = u * poly(SIN_C, w)
    c = poly(COS_C, w)
    return 1.0 - s * s, s * c


VMEM = pl.BlockSpec(memory_space=pltpu.VMEM)
SMALL = pltpu.CompilerParams(vmem_limit_bytes=16 << 20)


def on_chip(*values):
    return [pltpu.with_memory_space_constraint(v, pltpu.VMEM) for v in values]


def in_hbm(*values):
    return [pltpu.with_memory_space_constraint(v, pltpu.HBM) for v in values]


def pack_kernel(count_ref, _z, _slot, pos_ref, feats_ref, waves_ref, filt_ref, out_ref, waves_out, filt_out):
    rows = feats_ref.shape[0]
    waves = waves_ref[...].astype(f32)
    waves_out[...] = jnp.concatenate(
        [waves, waves, waves, jnp.zeros((7, waves.shape[1]), f32)], axis=0
    ).astype(bf16)
    filt_out[...] = filt_ref[...]
    slot = lax.broadcasted_iota(jnp.int32, feats_ref.shape, 0)
    live = slot < count_ref[0]
    feats = feats_ref[...].astype(f32)
    out_ref[0:rows, :] = jnp.where(live, feats, 0.0).astype(bf16)
    pos = pos_ref[...]
    hi = pos.astype(bf16).astype(f32)
    rest = pos - hi
    mid = rest.astype(bf16).astype(f32)
    low = rest - mid
    n = pos.shape[1]
    tail = jnp.concatenate([hi, mid, low, jnp.zeros((7, n), f32)], axis=0)
    out_ref[rows : rows + 16, :] = jnp.concatenate(
        [tail, jnp.zeros((16, feats.shape[1] - n), f32)], axis=1
    ).astype(bf16)


def pack(counts, z, slot, positions, feats, waves, wave_filter, share, own):
    rows, width = feats.shape

    def whole(v):
        return pl.BlockSpec(v.shape, lambda i, c, z, s: (0, 0))

    return pl.pallas_call(
        pack_kernel,
        grid_spec=pltpu.PrefetchScalarGridSpec(
            num_scalar_prefetch=3,
            grid=(1,),
            in_specs=[
                whole(positions),
                whole(feats),
                pl.BlockSpec((3, share), lambda i, c, z, s: (0, z[0])),
                pl.BlockSpec((own, width), lambda i, c, z, s: (s[0], 0)),
            ],
            out_specs=(
                pl.BlockSpec((rows + 16, width), lambda i, c, z, s: (0, 0)),
                pl.BlockSpec((16, share), lambda i, c, z, s: (0, 0)),
                pl.BlockSpec((own, width), lambda i, c, z, s: (0, 0)),
            ),
        ),
        out_shape=(
            jax.ShapeDtypeStruct((rows + 16, width), bf16),
            jax.ShapeDtypeStruct((16, share), bf16),
            jax.ShapeDtypeStruct((own, width), bf16),
        ),
        compiler_params=SMALL,
        name="pack_atoms",
    )(counts, z[None], slot[None], *in_hbm(positions, feats, waves, wave_filter))


OWN = 32
EXTRA = 16


def load_blocks(block_refs, layout, feats, coords):
    n = coords.shape[1] // len(layout)
    for j, (source, k) in enumerate(layout):
        block = block_refs[source]
        at = k * (n + EXTRA)
        if feats is not None:
            feats[j * n : (j + 1) * n, :] = block[at : at + n, :]
        coords[:, j * n : (j + 1) * n] = block[at + n : at + n + EXTRA, 0:n]


def fill_tile(waves_ref, coords, turns, tile_ref):
    rows, _ = turns.shape
    turns[...] = jnp.dot(
        waves_ref[...].astype(f32).T.astype(bf16), coords[...], preferred_element_type=f32
    )

    def step(i, carry):
        for h in range(0, OWN, 16):
            at = pl.ds(pl.multiple_of(i * OWN + h, 16), 16)
            to_cos = pl.ds(pl.multiple_of(i * 2 * OWN + h, 16), 16)
            to_sin = pl.ds(pl.multiple_of(i * 2 * OWN + OWN + h, 16), 16)
            c, s = cos_sin(turns[at, :])
            tile_ref[to_cos, :] = c.astype(bf16)
            tile_ref[to_sin, :] = s.astype(bf16)
        return carry

    lax.fori_loop(0, rows // OWN, step, 0, unroll=2)


def early_tiles(both_waves, blocks, layout):
    rows = both_waves[0].shape[1]
    n = blocks[0].shape[0] - EXTRA
    atoms = n * len(layout)
    nb = len(blocks)

    def kernel(*refs):
        out_a, out_b, coords, turns = refs[2 + nb :]
        load_blocks(refs[2 : 2 + nb], layout, None, coords)
        fill_tile(refs[0], coords, turns, out_a)
        fill_tile(refs[1], coords, turns, out_b)

    return pl.pallas_call(
        kernel,
        out_shape=(pltpu.VMEM((2 * rows, atoms), bf16),) * 2,
        in_specs=[VMEM] * (2 + nb),
        out_specs=(VMEM, VMEM),
        scratch_shapes=[pltpu.VMEM((EXTRA, atoms), bf16), pltpu.VMEM((rows, atoms), f32)],
        compiler_params=SMALL,
        cost_estimate=pl.CostEstimate(
            flops=1024 * rows * atoms, transcendentals=0, bytes_accessed=8 * rows * atoms
        ),
        name="early_tiles",
    )(*on_chip(*both_waves, *blocks))


def factors(waves9, tile, early, early_layout, late, late_layout, dtype):
    rows = waves9.shape[1]
    width = early[0].shape[1]
    n = early[0].shape[0] - EXTRA
    atoms = n * len(late_layout)
    ready = n * len(early_layout)
    groups = rows // OWN
    ne, nl = len(early), len(late)

    def kernel(*refs):
        waves_ref, ready_ref = refs[:2]
        early_refs = refs[2 : 2 + ne]
        late_refs = refs[2 + ne : 2 + ne + nl]
        out_ref, tile_ref, feats_a, feats_b, coords_a, coords_b, turns = refs[2 + ne + nl :]
        load_blocks(early_refs, early_layout, feats_a, coords_a)
        load_blocks(late_refs, late_layout, feats_b, coords_b)
        fill_tile(waves_ref, coords_b, turns, tile_ref)
        summed = jnp.dot(ready_ref[...], feats_a[...], preferred_element_type=f32)
        summed = summed + jnp.dot(tile_ref[...], feats_b[...], preferred_element_type=f32)
        out_ref[...] = summed.astype(dtype).reshape(groups, 2, OWN, width)

    return pl.pallas_call(
        kernel,
        out_shape=(
            pltpu.VMEM((groups, 2, OWN, width), dtype),
            pltpu.VMEM((2 * rows, atoms), bf16),
        ),
        in_specs=[VMEM] * (2 + ne + nl),
        out_specs=(VMEM, VMEM),
        scratch_shapes=[
            pltpu.VMEM((ready, width), bf16),
            pltpu.VMEM((atoms, width), bf16),
            pltpu.VMEM((EXTRA, ready), bf16),
            pltpu.VMEM((EXTRA, atoms), bf16),
            pltpu.VMEM((rows, atoms), f32),
        ],
        compiler_params=SMALL,
        cost_estimate=pl.CostEstimate(
            flops=8 * rows * atoms * width, transcendentals=0, bytes_accessed=8 * rows * atoms
        ),
        name="structure_factors",
    )(*on_chip(waves9, tile, *early, *late))


def filter_kernel(arrived_ref, filt_ref, mix_ref, out_ref, *, scale):
    n = arrived_ref.shape[0]
    total = arrived_ref[0].astype(f32)
    for j in range(1, n):
        total = total + arrived_ref[j].astype(f32)
    filt = filt_ref[...].astype(f32)
    both = jnp.concatenate([total[0] * scale * filt, total[1] * scale * filt], axis=0)
    mixed = jnp.dot(
        both, mix_ref[...], precision=lax.Precision.HIGHEST, preferred_element_type=f32
    ).astype(bf16)
    rows = filt.shape[0]
    for j in range(n):
        out_ref[j, 0] = mixed[:rows]
        out_ref[j, 1] = mixed[rows:]


def filter_mix(arrived, filt, mixing, scale):
    return pl.pallas_call(
        lambda *refs: filter_kernel(*refs, scale=scale),
        out_shape=pltpu.VMEM(arrived.shape, bf16),
        in_specs=[VMEM] * 3,
        out_specs=VMEM,
        compiler_params=SMALL,
        name="filter_mix",
    )(*on_chip(arrived, filt, mixing))


def fields(tiles, halves, outs, after=()):
    owners, two, own, width = halves[0].shape
    half = owners * two * own
    n = 128
    wanted = [place for places, _ in outs for place in places]
    first = min(j for _, j in wanted)
    last = max(j for _, j in wanted) + 1

    def kernel(*refs):
        tile_refs, half_refs = refs[:4], refs[4:6]
        out_refs = refs[6 + len(after) :]
        left = [f[...].reshape(half, width).T for f in half_refs]
        got = []
        for t in range(2):
            field = None
            for h in range(2):
                part = jnp.dot(
                    left[h],
                    tile_refs[2 * h + t][:, first * n : last * n],
                    preferred_element_type=f32,
                )
                field = part if field is None else field + part
            got.append(field)
        for out, (places, dtype) in zip(out_refs, outs):
            for k, (t, j) in enumerate(places):
                at = (j - first) * n
                out[k] = got[t][:, at : at + n].astype(dtype)

    return pl.pallas_call(
        kernel,
        out_shape=tuple(pltpu.VMEM((len(places), width, n), d) for places, d in outs),
        in_specs=[VMEM] * 6 + [pl.BlockSpec(memory_space=pl.ANY)] * len(after),
        out_specs=(VMEM,) * len(outs),
        compiler_params=SMALL,
        cost_estimate=pl.CostEstimate(
            flops=4 * half * width * n * len(wanted),
            transcendentals=0,
            bytes_accessed=4 * half * n * len(wanted),
        ),
        name="wave_fields",
    )(*on_chip(*tiles, *halves), *after)


def update_kernel(count_ref, *refs, scale):
    part_refs = refs[:-5]
    feats_ref, gain_ref, win_ref, wout_ref, out_ref = refs[-5:]
    total = part_refs[0][0].astype(f32)
    for part in part_refs[1:]:
        total = total + part[0].astype(f32)
    state = feats_ref[...].astype(f32) + (total * scale).T
    meansq = jnp.mean(state * state, axis=1, keepdims=True)
    normed = (state * lax.rsqrt(meansq + 1e-06) * gain_ref[...]).astype(bf16)
    v = jnp.dot(normed, win_ref[...], preferred_element_type=f32)
    hidden = (v / (1.0 + jnp.exp(-v))).astype(bf16)
    result = state + jnp.dot(hidden, wout_ref[...], preferred_element_type=f32)
    slot = lax.broadcasted_iota(jnp.int32, result.shape, 0)
    out_ref[...] = jnp.where(slot < count_ref[0], result, 0.0).astype(bf16)


def update(counts, parts, feats, gain, w_in, w_out, scale):
    return pl.pallas_call(
        lambda *refs: update_kernel(*refs, scale=scale),
        out_shape=jax.ShapeDtypeStruct(feats.shape, bf16),
        in_specs=[pl.BlockSpec(memory_space=pltpu.SMEM)] + [VMEM] * (len(parts) + 4),
        out_specs=VMEM,
        compiler_params=SMALL,
        name="update_atoms",
    )(counts, *on_chip(*parts, feats, gain[None, :], w_in, w_out))


def layer(positions, counts, feats, waves, wave_filter, mixing, gain, w_in, w_out):
    kw = waves.shape[1]
    share = kw // NZ
    own_waves = share // NYX
    atoms_all = feats.shape[0] * NZ * NYX * NC
    kwaves_all = kw * NC
    z = lax.axis_index("z")
    yx = lax.axis_index("y") * NX + lax.axis_index("x")
    swap = [(0, 1), (1, 0)]

    def partner(v):
        return lax.ppermute(v, "core", swap)

    def shift(v, d):
        return lax.ppermute(v, "z", [(i, (i + d) % NZ) for i in range(NZ)]) if d else v

    def exchange(v):
        return lax.all_to_all(v, ("y", "x"), 0, 0, tiled=True)

    block, mine, filt = pack(
        counts, z, z * NYX + yx, positions, feats, waves, wave_filter, share, own_waves
    )
    other = partner(mine)
    opposite = shift(block, HALF)
    ahead = shift(block, -2)
    behind = shift(block, 2)
    pair = jnp.concatenate([block, opposite], axis=0)
    near_behind = shift(pair, 1)
    near_ahead = shift(pair, -1)
    early = [ahead, behind, opposite, block]
    early_layout = [(0, 0), (1, 0), (2, 0), (3, 0)]
    late = [near_behind, near_ahead]
    late_layout = [(0, 1), (1, 1), (1, 0), (0, 0)]
    ready_other, ready_mine = early_tiles([other, mine], early, early_layout)
    sent, tile_other = factors(other, ready_other, early, early_layout, late, late_layout, bf16)
    arrived = partner(sent)
    kept, tile_mine = factors(mine, ready_mine, early, early_layout, late, late_layout, f32)
    summed = exchange((kept + arrived.astype(f32)).astype(bf16))
    spread = filter_mix(summed, filt, mixing, 1.0 / math.sqrt(atoms_all))
    filtered = exchange(spread)
    halves = (partner(filtered), filtered)

    tiles = (ready_other, tile_other, ready_mine, tile_mine)
    to_ahead, to_behind = fields(
        tiles, halves, [([(0, 0), (1, 0)], bf16), ([(0, 1), (1, 1)], bf16)]
    )
    far, own, one_ahead, one_behind = fields(
        tiles,
        halves,
        [([(0, 2)], bf16), ([(0, 3)], f32), ([(1, 2)], f32), ([(1, 3)], f32)],
        (to_ahead,),
    )
    from_behind = shift(to_ahead, 2)
    from_ahead = shift(to_behind, -2)
    opposite = shift(far, HALF)
    one_ahead = (one_ahead + from_behind[1:].astype(f32)).astype(bf16)
    one_behind = (one_behind + from_ahead[1:].astype(f32)).astype(bf16)
    near_behind = shift(one_ahead, 1)
    near_ahead = shift(one_behind, -1)
    parts = [own, from_ahead, from_behind, opposite, near_behind, near_ahead]
    return update(counts, parts, feats, gain, w_in, w_out, 1.0 / math.sqrt(kwaves_all))


def solution(mesh):
    fine = Mesh(mesh.devices.reshape(NZ, NY, NX, NC), ("z", "y", "x", "core"))
    every = ("z", "y", "x", "core")
    return jax.shard_map(
        layer,
        mesh=fine,
        in_specs=(
            P(None, every),
            P(every),
            P(every, None),
            P(None, "core"),
            P("core", None),
            P(),
            P(),
            P(),
            P(),
        ),
        out_specs=P(every, None),
        check_vma=False,
    )
```

```python
import math

import jax
import jax.numpy as jnp
from jax import lax
from jax.experimental import pallas as pl
from jax.experimental.pallas import tpu as pltpu
from jax.sharding import Mesh
from jax.sharding import PartitionSpec as P

bf16 = jnp.bfloat16
f32 = jnp.float32

NZ, NY, NX, NC = 8, 4, 4, 2
NYX = NY * NX
HALF = NZ // 2


ROOT2 = math.sqrt(2.0)
SIN_C = (
    3.1415926520468305,
    -5.167710734303894,
    2.550084223872135,
    -0.5983094608569061,
    0.07765872505863924,
)
COS_C = (
    0.9999999946405678,
    -4.934795092504032,
    4.058434665884265,
    -1.3319399977127386,
    0.21969398917152252,
)
MAGIC = 1.5 * 2.0**23


def poly(coefs, w):
    acc = coefs[-1] * ROOT2
    for c in coefs[-2::-1]:
        acc = acc * w + c * ROOT2
    return acc


def cos_sin(turns):
    u = turns - ((turns + MAGIC) - MAGIC)
    w = u * u
    s = u * poly(SIN_C, w)
    c = poly(COS_C, w)
    return 1.0 - s * s, s * c


VMEM = pl.BlockSpec(memory_space=pltpu.VMEM)
SMALL = pltpu.CompilerParams(vmem_limit_bytes=16 << 20)


def on_chip(*values):
    return [pltpu.with_memory_space_constraint(v, pltpu.VMEM) for v in values]


def in_hbm(*values):
    return [pltpu.with_memory_space_constraint(v, pltpu.HBM) for v in values]


def pack_kernel(count_ref, _z, _slot, pos_ref, feats_ref, waves_ref, filt_ref, out_ref, waves_out, filt_out):
    rows = feats_ref.shape[0]
    waves = waves_ref[...].astype(f32)
    waves_out[...] = jnp.concatenate(
        [waves, waves, waves, jnp.zeros((7, waves.shape[1]), f32)], axis=0
    ).astype(bf16)
    filt_out[...] = filt_ref[...]
    slot = lax.broadcasted_iota(jnp.int32, feats_ref.shape, 0)
    live = slot < count_ref[0]
    feats = feats_ref[...].astype(f32)
    out_ref[0:rows, :] = jnp.where(live, feats, 0.0).astype(bf16)
    pos = pos_ref[...]
    hi = pos.astype(bf16).astype(f32)
    rest = pos - hi
    mid = rest.astype(bf16).astype(f32)
    low = rest - mid
    n = pos.shape[1]
    tail = jnp.concatenate([hi, mid, low, jnp.zeros((7, n), f32)], axis=0)
    out_ref[rows : rows + 16, :] = jnp.concatenate(
        [tail, jnp.zeros((16, feats.shape[1] - n), f32)], axis=1
    ).astype(bf16)


def pack(counts, z, slot, positions, feats, waves, wave_filter, share, own):
    rows, width = feats.shape

    def whole(v):
        return pl.BlockSpec(v.shape, lambda i, c, z, s: (0, 0))

    return pl.pallas_call(
        pack_kernel,
        grid_spec=pltpu.PrefetchScalarGridSpec(
            num_scalar_prefetch=3,
            grid=(1,),
            in_specs=[
                whole(positions),
                whole(feats),
                pl.BlockSpec((3, share), lambda i, c, z, s: (0, z[0])),
                pl.BlockSpec((own, width), lambda i, c, z, s: (s[0], 0)),
            ],
            out_specs=(
                pl.BlockSpec((rows + 16, width), lambda i, c, z, s: (0, 0)),
                pl.BlockSpec((16, share), lambda i, c, z, s: (0, 0)),
                pl.BlockSpec((own, width), lambda i, c, z, s: (0, 0)),
            ),
        ),
        out_shape=(
            jax.ShapeDtypeStruct((rows + 16, width), bf16),
            jax.ShapeDtypeStruct((16, share), bf16),
            jax.ShapeDtypeStruct((own, width), bf16),
        ),
        compiler_params=SMALL,
        name="pack_atoms",
    )(counts, z[None], slot[None], *in_hbm(positions, feats, waves, wave_filter))


OWN = 32
EXTRA = 16


def load_blocks(block_refs, layout, feats, coords):
    n = coords.shape[1] // len(layout)
    for j, (source, k) in enumerate(layout):
        block = block_refs[source]
        at = k * (n + EXTRA)
        feats[j * n : (j + 1) * n, :] = block[at : at + n, :]
        coords[:, j * n : (j + 1) * n] = block[at + n : at + n + EXTRA, 0:n]


def fill_tile(waves_ref, coords, turns, tile_ref):
    rows, _ = turns.shape
    turns[...] = jnp.dot(
        waves_ref[...].astype(f32).T.astype(bf16), coords[...], preferred_element_type=f32
    )

    def step(i, carry):
        for h in range(0, OWN, 16):
            at = pl.ds(pl.multiple_of(i * OWN + h, 16), 16)
            to_cos = pl.ds(pl.multiple_of(i * 2 * OWN + h, 16), 16)
            to_sin = pl.ds(pl.multiple_of(i * 2 * OWN + OWN + h, 16), 16)
            c, s = cos_sin(turns[at, :])
            tile_ref[to_cos, :] = c.astype(bf16)
            tile_ref[to_sin, :] = s.astype(bf16)
        return carry

    lax.fori_loop(0, rows // OWN, step, 0, unroll=2)


def early_factors(both_waves, blocks, layout):
    rows = both_waves[0].shape[1]
    width = blocks[0].shape[1]
    n = blocks[0].shape[0] - EXTRA
    atoms = n * len(layout)
    nb = len(blocks)

    def kernel(*refs):
        tile_refs, sum_refs = refs[2 + nb : 4 + nb], refs[4 + nb : 6 + nb]
        feats, coords, turns = refs[6 + nb :]
        load_blocks(refs[2 : 2 + nb], layout, feats, coords)
        for waves_ref, tile_ref, sum_ref in zip(refs[:2], tile_refs, sum_refs):
            fill_tile(waves_ref, coords, turns, tile_ref)
            sum_ref[...] = jnp.dot(tile_ref[...], feats[...], preferred_element_type=f32)

    tile = pltpu.VMEM((2 * rows, atoms), bf16)
    part = pltpu.VMEM((2 * rows, width), f32)
    return pl.pallas_call(
        kernel,
        out_shape=(tile, tile, part, part),
        in_specs=[VMEM] * (2 + nb),
        out_specs=(VMEM,) * 4,
        scratch_shapes=[
            pltpu.VMEM((atoms, width), bf16),
            pltpu.VMEM((EXTRA, atoms), bf16),
            pltpu.VMEM((rows, atoms), f32),
        ],
        compiler_params=SMALL,
        cost_estimate=pl.CostEstimate(
            flops=8 * rows * atoms * width, transcendentals=0, bytes_accessed=8 * rows * atoms
        ),
        name="early_factors",
    )(*on_chip(*both_waves, *blocks))


def factors(waves9, part, late, layout, dtype):
    rows = waves9.shape[1]
    width = late[0].shape[1]
    n = sum(b.shape[0] for b in late) // len(layout) - EXTRA
    atoms = n * len(layout)
    groups = rows // OWN
    nl = len(late)

    def kernel(*refs):
        waves_ref, part_ref = refs[:2]
        out_ref, tile_ref, feats, coords, turns = refs[2 + nl :]
        load_blocks(refs[2 : 2 + nl], layout, feats, coords)
        fill_tile(waves_ref, coords, turns, tile_ref)
        summed = jnp.dot(tile_ref[...], feats[...], preferred_element_type=f32)
        summed = summed + part_ref[...]
        out_ref[...] = summed.astype(dtype).reshape(groups, 2, OWN, width)

    return pl.pallas_call(
        kernel,
        out_shape=(
            pltpu.VMEM((groups, 2, OWN, width), dtype),
            pltpu.VMEM((2 * rows, atoms), bf16),
        ),
        in_specs=[VMEM] * (2 + nl),
        out_specs=(VMEM, VMEM),
        scratch_shapes=[
            pltpu.VMEM((atoms, width), bf16),
            pltpu.VMEM((EXTRA, atoms), bf16),
            pltpu.VMEM((rows, atoms), f32),
        ],
        compiler_params=SMALL,
        cost_estimate=pl.CostEstimate(
            flops=4 * rows * atoms * width, transcendentals=0, bytes_accessed=8 * rows * atoms
        ),
        name="structure_factors",
    )(*on_chip(waves9, part, *late))


def filter_kernel(arrived_ref, filt_ref, mix_ref, out_ref, *, scale):
    n = arrived_ref.shape[0]
    total = arrived_ref[0].astype(f32)
    for j in range(1, n):
        total = total + arrived_ref[j].astype(f32)
    filt = filt_ref[...].astype(f32)
    both = jnp.concatenate([total[0] * scale * filt, total[1] * scale * filt], axis=0)
    mixed = jnp.dot(
        both, mix_ref[...], precision=lax.Precision.HIGHEST, preferred_element_type=f32
    ).astype(bf16)
    rows = filt.shape[0]
    for j in range(n):
        out_ref[j, 0] = mixed[:rows]
        out_ref[j, 1] = mixed[rows:]


def filter_mix(arrived, filt, mixing, scale):
    return pl.pallas_call(
        lambda *refs: filter_kernel(*refs, scale=scale),
        out_shape=pltpu.VMEM(arrived.shape, bf16),
        in_specs=[VMEM] * 3,
        out_specs=VMEM,
        compiler_params=SMALL,
        name="filter_mix",
    )(*on_chip(arrived, filt, mixing))


def own_fields(tiles, half_of):
    owners, two, own, width = half_of.shape
    half = owners * two * own

    def kernel(early_ref, late_ref, f_ref, early_out, late_out):
        left = f_ref[...].reshape(half, width).T
        early_out[...] = jnp.dot(left, early_ref[...], preferred_element_type=f32)
        late_out[...] = jnp.dot(left, late_ref[...], preferred_element_type=f32)

    return pl.pallas_call(
        kernel,
        out_shape=tuple(pltpu.VMEM((width, t.shape[1]), f32) for t in tiles),
        in_specs=[VMEM] * 3,
        out_specs=(VMEM,) * 2,
        compiler_params=SMALL,
        cost_estimate=pl.CostEstimate(
            flops=4 * half * width * tiles[0].shape[1],
            transcendentals=0,
            bytes_accessed=4 * half * tiles[0].shape[1],
        ),
        name="own_fields",
    )(*on_chip(*tiles, half_of))


def fields(tiles, half_of, ready, outs):
    owners, two, own, width = half_of.shape
    half = owners * two * own
    n = 128

    def kernel(*refs):
        tile_refs, f_ref, ready_refs = refs[:2], refs[2], refs[3:5]
        left = f_ref[...].reshape(half, width).T
        got = [
            jnp.dot(left, tile[...], preferred_element_type=f32) + before[...]
            for tile, before in zip(tile_refs, ready_refs)
        ]
        for out, (places, dtype) in zip(refs[5:], outs):
            for k, (t, j) in enumerate(places):
                out[k] = got[t][:, j * n : (j + 1) * n].astype(dtype)

    return pl.pallas_call(
        kernel,
        out_shape=tuple(pltpu.VMEM((len(places), width, n), d) for places, d in outs),
        in_specs=[VMEM] * 5,
        out_specs=(VMEM,) * len(outs),
        compiler_params=SMALL,
        cost_estimate=pl.CostEstimate(
            flops=4 * half * width * tiles[0].shape[1],
            transcendentals=0,
            bytes_accessed=4 * half * tiles[0].shape[1],
        ),
        name="wave_fields",
    )(*on_chip(*tiles, half_of, *ready))


def update_kernel(count_ref, *refs, scale):
    part_refs = refs[:-5]
    feats_ref, gain_ref, win_ref, wout_ref, out_ref = refs[-5:]
    total = part_refs[0][0].astype(f32)
    for part in part_refs[1:]:
        total = total + part[0].astype(f32)
    state = feats_ref[...].astype(f32) + (total * scale).T
    meansq = jnp.mean(state * state, axis=1, keepdims=True)
    normed = (state * lax.rsqrt(meansq + 1e-06) * gain_ref[...]).astype(bf16)
    v = jnp.dot(normed, win_ref[...], preferred_element_type=f32)
    hidden = (v / (1.0 + jnp.exp(-v))).astype(bf16)
    result = state + jnp.dot(hidden, wout_ref[...], preferred_element_type=f32)
    slot = lax.broadcasted_iota(jnp.int32, result.shape, 0)
    out_ref[...] = jnp.where(slot < count_ref[0], result, 0.0).astype(bf16)


def update(counts, parts, feats, gain, w_in, w_out, scale):
    return pl.pallas_call(
        lambda *refs: update_kernel(*refs, scale=scale),
        out_shape=jax.ShapeDtypeStruct(feats.shape, bf16),
        in_specs=[pl.BlockSpec(memory_space=pltpu.SMEM)] + [VMEM] * (len(parts) + 4),
        out_specs=VMEM,
        compiler_params=SMALL,
        name="update_atoms",
    )(counts, *on_chip(*parts, feats, gain[None, :], w_in, w_out))


def layer(positions, counts, feats, waves, wave_filter, mixing, gain, w_in, w_out):
    kw = waves.shape[1]
    share = kw // NZ
    own_waves = share // NYX
    atoms_all = feats.shape[0] * NZ * NYX * NC
    kwaves_all = kw * NC
    z = lax.axis_index("z")
    yx = lax.axis_index("y") * NX + lax.axis_index("x")
    swap = [(0, 1), (1, 0)]

    def partner(v):
        return lax.ppermute(v, "core", swap)

    def shift(v, d):
        return lax.ppermute(v, "z", [(i, (i + d) % NZ) for i in range(NZ)]) if d else v

    def exchange(v):
        return lax.all_to_all(v, ("y", "x"), 0, 0, tiled=True)

    block, mine, filt = pack(
        counts, z, z * NYX + yx, positions, feats, waves, wave_filter, share, own_waves
    )
    other = partner(mine)
    opposite = shift(block, HALF)
    ahead = shift(block, -2)
    behind = shift(block, 2)
    pair = jnp.concatenate([block, opposite], axis=0)
    near_behind = shift(pair, 1)
    near_ahead = shift(pair, -1)
    early = [ahead, behind, opposite, block]
    early_layout = [(0, 0), (1, 0), (2, 0), (3, 0)]
    late = [near_behind, near_ahead]
    late_layout = [(0, 1), (1, 1), (1, 0), (0, 0)]
    ready_other, ready_mine, part_other, part_mine = early_factors(
        [other, mine], early, early_layout
    )
    sent, tile_other = factors(other, part_other, late, late_layout, bf16)
    arrived = partner(sent)
    kept, tile_mine = factors(mine, part_mine, late, late_layout, f32)
    summed = exchange((kept + arrived.astype(f32)).astype(bf16))
    spread = filter_mix(summed, filt, mixing, 1.0 / math.sqrt(atoms_all))
    filtered = exchange(spread)
    filtered_other = partner(filtered)
    ready = own_fields((ready_mine, tile_mine), filtered)
    to_ahead, to_behind, far, own, one_ahead, one_behind = fields(
        (ready_other, tile_other),
        filtered_other,
        ready,
        [
            ([(0, 0), (1, 0)], bf16),
            ([(0, 1), (1, 1)], bf16),
            ([(0, 2)], bf16),
            ([(0, 3)], f32),
            ([(1, 2)], f32),
            ([(1, 3)], f32),
        ],
    )
    from_behind = shift(to_ahead, 2)
    from_ahead = shift(to_behind, -2)
    opposite = shift(far, HALF)
    one_ahead = (one_ahead + from_behind[1:].astype(f32)).astype(bf16)
    one_behind = (one_behind + from_ahead[1:].astype(f32)).astype(bf16)
    near_behind = shift(one_ahead, 1)
    near_ahead = shift(one_behind, -1)
    parts = [own, from_ahead, from_behind, opposite, near_behind, near_ahead]
    return update(counts, parts, feats, gain, w_in, w_out, 1.0 / math.sqrt(kwaves_all))


def solution(mesh):
    fine = Mesh(mesh.devices.reshape(NZ, NY, NX, NC), ("z", "y", "x", "core"))
    every = ("z", "y", "x", "core")
    return jax.shard_map(
        layer,
        mesh=fine,
        in_specs=(
            P(None, every),
            P(every),
            P(every, None),
            P(None, "core"),
            P("core", None),
            P(),
            P(),
            P(),
            P(),
        ),
        out_specs=P(every, None),
        check_vma=False,
    )
```

```python
import math

import jax
import jax.numpy as jnp
from jax import lax
from jax.experimental import pallas as pl
from jax.experimental.pallas import tpu as pltpu
from jax.sharding import Mesh
from jax.sharding import PartitionSpec as P

bf16 = jnp.bfloat16
f32 = jnp.float32

NZ, NY, NX, NC = 8, 4, 4, 2
NYX = NY * NX
HALF = NZ // 2


ROOT2 = math.sqrt(2.0)
SIN_C = (
    3.1415926520468305,
    -5.167710734303894,
    2.550084223872135,
    -0.5983094608569061,
    0.07765872505863924,
)
COS_C = (
    0.9999999946405678,
    -4.934795092504032,
    4.058434665884265,
    -1.3319399977127386,
    0.21969398917152252,
)
MAGIC = 1.5 * 2.0**23


def poly(coefs, w):
    acc = coefs[-1] * ROOT2
    for c in coefs[-2::-1]:
        acc = acc * w + c * ROOT2
    return acc


def cos_sin(turns):
    u = turns - ((turns + MAGIC) - MAGIC)
    w = u * u
    s = u * poly(SIN_C, w)
    c = poly(COS_C, w)
    return 1.0 - s * s, s * c


VMEM = pl.BlockSpec(memory_space=pltpu.VMEM)
SMALL = pltpu.CompilerParams(vmem_limit_bytes=16 << 20)


def on_chip(*values):
    return [pltpu.with_memory_space_constraint(v, pltpu.VMEM) for v in values]


def in_hbm(*values):
    return [pltpu.with_memory_space_constraint(v, pltpu.HBM) for v in values]


def pack_kernel(count_ref, _z, _slot, pos_ref, feats_ref, waves_ref, filt_ref, out_ref, waves_out, filt_out):
    rows = feats_ref.shape[0]
    waves = waves_ref[...].astype(f32)
    waves_out[...] = jnp.concatenate(
        [waves, waves, waves, jnp.zeros((7, waves.shape[1]), f32)], axis=0
    ).astype(bf16)
    filt_out[...] = filt_ref[...]
    slot = lax.broadcasted_iota(jnp.int32, feats_ref.shape, 0)
    live = slot < count_ref[0]
    feats = feats_ref[...].astype(f32)
    out_ref[0:rows, :] = jnp.where(live, feats, 0.0).astype(bf16)
    pos = pos_ref[...]
    hi = pos.astype(bf16).astype(f32)
    rest = pos - hi
    mid = rest.astype(bf16).astype(f32)
    low = rest - mid
    n = pos.shape[1]
    tail = jnp.concatenate([hi, mid, low, jnp.zeros((7, n), f32)], axis=0)
    out_ref[rows : rows + 16, :] = jnp.concatenate(
        [tail, jnp.zeros((16, feats.shape[1] - n), f32)], axis=1
    ).astype(bf16)


def pack(counts, z, slot, positions, feats, waves, wave_filter, share, own):
    rows, width = feats.shape

    def whole(v):
        return pl.BlockSpec(v.shape, lambda i, c, z, s: (0, 0))

    return pl.pallas_call(
        pack_kernel,
        grid_spec=pltpu.PrefetchScalarGridSpec(
            num_scalar_prefetch=3,
            grid=(1,),
            in_specs=[
                whole(positions),
                whole(feats),
                pl.BlockSpec((3, share), lambda i, c, z, s: (0, z[0])),
                pl.BlockSpec((own, width), lambda i, c, z, s: (s[0], 0)),
            ],
            out_specs=(
                pl.BlockSpec((rows + 16, width), lambda i, c, z, s: (0, 0)),
                pl.BlockSpec((16, share), lambda i, c, z, s: (0, 0)),
                pl.BlockSpec((own, width), lambda i, c, z, s: (0, 0)),
            ),
        ),
        out_shape=(
            jax.ShapeDtypeStruct((rows + 16, width), bf16),
            jax.ShapeDtypeStruct((16, share), bf16),
            jax.ShapeDtypeStruct((own, width), bf16),
        ),
        compiler_params=SMALL,
        name="pack_atoms",
    )(counts, z[None], slot[None], *in_hbm(positions, feats, waves, wave_filter))


OWN = 32
EXTRA = 16


def load_blocks(block_refs, layout, feats, coords):
    n = coords.shape[1] // len(layout)
    for j, (source, k) in enumerate(layout):
        block = block_refs[source]
        at = k * (n + EXTRA)
        feats[j * n : (j + 1) * n, :] = block[at : at + n, :]
        coords[:, j * n : (j + 1) * n] = block[at + n : at + n + EXTRA, 0:n]


def fill_tile(waves_ref, coords, turns, tile_ref):
    rows, _ = turns.shape
    turns[...] = jnp.dot(
        waves_ref[...].astype(f32).T.astype(bf16), coords[...], preferred_element_type=f32
    )

    def step(i, carry):
        for h in range(0, OWN, 16):
            at = pl.ds(pl.multiple_of(i * OWN + h, 16), 16)
            to_cos = pl.ds(pl.multiple_of(i * 2 * OWN + h, 16), 16)
            to_sin = pl.ds(pl.multiple_of(i * 2 * OWN + OWN + h, 16), 16)
            c, s = cos_sin(turns[at, :])
            tile_ref[to_cos, :] = c.astype(bf16)
            tile_ref[to_sin, :] = s.astype(bf16)
        return carry

    lax.fori_loop(0, rows // OWN, step, 0, unroll=4)


def early_factors(both_waves, blocks, layout):
    rows = both_waves[0].shape[1]
    width = blocks[0].shape[1]
    n = blocks[0].shape[0] - EXTRA
    atoms = n * len(layout)
    nb = len(blocks)

    def kernel(*refs):
        tile_refs, sum_refs = refs[2 + nb : 4 + nb], refs[4 + nb : 6 + nb]
        feats, coords, turns = refs[6 + nb :]
        load_blocks(refs[2 : 2 + nb], layout, feats, coords)
        for waves_ref, tile_ref, sum_ref in zip(refs[:2], tile_refs, sum_refs):
            fill_tile(waves_ref, coords, turns, tile_ref)
            sum_ref[...] = jnp.dot(tile_ref[...], feats[...], preferred_element_type=f32)

    tile = pltpu.VMEM((2 * rows, atoms), bf16)
    part = pltpu.VMEM((2 * rows, width), f32)
    return pl.pallas_call(
        kernel,
        out_shape=(tile, tile, part, part),
        in_specs=[VMEM] * (2 + nb),
        out_specs=(VMEM,) * 4,
        scratch_shapes=[
            pltpu.VMEM((atoms, width), bf16),
            pltpu.VMEM((EXTRA, atoms), bf16),
            pltpu.VMEM((rows, atoms), f32),
        ],
        compiler_params=SMALL,
        cost_estimate=pl.CostEstimate(
            flops=8 * rows * atoms * width, transcendentals=0, bytes_accessed=8 * rows * atoms
        ),
        name="early_factors",
    )(*on_chip(*both_waves, *blocks))


def factors(waves9, part, late, layout, dtype):
    rows = waves9.shape[1]
    width = late[0].shape[1]
    n = sum(b.shape[0] for b in late) // len(layout) - EXTRA
    atoms = n * len(layout)
    groups = rows // OWN
    nl = len(late)

    def kernel(*refs):
        waves_ref, part_ref = refs[:2]
        out_ref, tile_ref, feats, coords, turns = refs[2 + nl :]
        load_blocks(refs[2 : 2 + nl], layout, feats, coords)
        fill_tile(waves_ref, coords, turns, tile_ref)
        summed = jnp.dot(tile_ref[...], feats[...], preferred_element_type=f32)
        summed = summed + part_ref[...]
        out_ref[...] = summed.astype(dtype).reshape(groups, 2, OWN, width)

    return pl.pallas_call(
        kernel,
        out_shape=(
            pltpu.VMEM((groups, 2, OWN, width), dtype),
            pltpu.VMEM((2 * rows, atoms), bf16),
        ),
        in_specs=[VMEM] * (2 + nl),
        out_specs=(VMEM, VMEM),
        scratch_shapes=[
            pltpu.VMEM((atoms, width), bf16),
            pltpu.VMEM((EXTRA, atoms), bf16),
            pltpu.VMEM((rows, atoms), f32),
        ],
        compiler_params=SMALL,
        cost_estimate=pl.CostEstimate(
            flops=4 * rows * atoms * width, transcendentals=0, bytes_accessed=8 * rows * atoms
        ),
        name="structure_factors",
    )(*on_chip(waves9, part, *late))


def filter_kernel(arrived_ref, filt_ref, mix_ref, out_ref, *, scale):
    n = arrived_ref.shape[0]
    total = arrived_ref[0].astype(f32)
    for j in range(1, n):
        total = total + arrived_ref[j].astype(f32)
    filt = filt_ref[...].astype(f32)
    both = jnp.concatenate([total[0] * scale * filt, total[1] * scale * filt], axis=0)
    mixed = jnp.dot(
        both, mix_ref[...], precision=lax.Precision.HIGHEST, preferred_element_type=f32
    ).astype(bf16)
    rows = filt.shape[0]
    for j in range(n):
        out_ref[j, 0] = mixed[:rows]
        out_ref[j, 1] = mixed[rows:]


def filter_mix(arrived, filt, mixing, scale):
    return pl.pallas_call(
        lambda *refs: filter_kernel(*refs, scale=scale),
        out_shape=pltpu.VMEM(arrived.shape, bf16),
        in_specs=[VMEM] * 3,
        out_specs=VMEM,
        compiler_params=SMALL,
        name="filter_mix",
    )(*on_chip(arrived, filt, mixing))


def own_fields(tiles, half_of):
    owners, two, own, width = half_of.shape
    half = owners * two * own

    def kernel(early_ref, late_ref, f_ref, early_out, late_out):
        left = f_ref[...].reshape(half, width).T
        early_out[...] = jnp.dot(left, early_ref[...], preferred_element_type=f32)
        late_out[...] = jnp.dot(left, late_ref[...], preferred_element_type=f32)

    return pl.pallas_call(
        kernel,
        out_shape=tuple(pltpu.VMEM((width, t.shape[1]), f32) for t in tiles),
        in_specs=[VMEM] * 3,
        out_specs=(VMEM,) * 2,
        compiler_params=SMALL,
        cost_estimate=pl.CostEstimate(
            flops=4 * half * width * tiles[0].shape[1],
            transcendentals=0,
            bytes_accessed=4 * half * tiles[0].shape[1],
        ),
        name="own_fields",
    )(*on_chip(*tiles, half_of))


def fields(tiles, half_of, ready, outs):
    owners, two, own, width = half_of.shape
    half = owners * two * own
    n = 128

    def kernel(*refs):
        tile_refs, f_ref, ready_refs = refs[:2], refs[2], refs[3:5]
        left = f_ref[...].reshape(half, width).T
        got = [
            jnp.dot(left, tile[...], preferred_element_type=f32) + before[...]
            for tile, before in zip(tile_refs, ready_refs)
        ]
        for out, (places, dtype) in zip(refs[5:], outs):
            for k, (t, j) in enumerate(places):
                out[k] = got[t][:, j * n : (j + 1) * n].astype(dtype)

    return pl.pallas_call(
        kernel,
        out_shape=tuple(pltpu.VMEM((len(places), width, n), d) for places, d in outs),
        in_specs=[VMEM] * 5,
        out_specs=(VMEM,) * len(outs),
        compiler_params=SMALL,
        cost_estimate=pl.CostEstimate(
            flops=4 * half * width * tiles[0].shape[1],
            transcendentals=0,
            bytes_accessed=4 * half * tiles[0].shape[1],
        ),
        name="wave_fields",
    )(*on_chip(*tiles, half_of, *ready))


def early_state_kernel(*refs, scale):
    part_refs, feats_ref, out_ref = refs[:-2], refs[-2], refs[-1]
    total = part_refs[0][0].astype(f32)
    for part in part_refs[1:]:
        total = total + part[0].astype(f32)
    out_ref[...] = feats_ref[...].astype(f32) + (total * scale).T


def early_state(parts, feats, scale):
    return pl.pallas_call(
        lambda *refs: early_state_kernel(*refs, scale=scale),
        out_shape=pltpu.VMEM(feats.shape, f32),
        in_specs=[VMEM] * (len(parts) + 1),
        out_specs=VMEM,
        compiler_params=SMALL,
        name="early_state",
    )(*on_chip(*parts, feats))


def update_kernel(count_ref, near_a, near_b, state_ref, gain_ref, win_ref, wout_ref, out_ref, *, scale):
    near = near_a[0].astype(f32) + near_b[0].astype(f32)
    state = state_ref[...] + (near * scale).T
    meansq = jnp.mean(state * state, axis=1, keepdims=True)
    normed = (state * lax.rsqrt(meansq + 1e-06) * gain_ref[...]).astype(bf16)
    v = jnp.dot(normed, win_ref[...], preferred_element_type=f32)
    hidden = (v / (1.0 + jnp.exp(-v))).astype(bf16)
    result = state + jnp.dot(hidden, wout_ref[...], preferred_element_type=f32)
    slot = lax.broadcasted_iota(jnp.int32, result.shape, 0)
    out_ref[...] = jnp.where(slot < count_ref[0], result, 0.0).astype(bf16)


def update(counts, near, state, gain, w_in, w_out, scale):
    return pl.pallas_call(
        lambda *refs: update_kernel(*refs, scale=scale),
        out_shape=jax.ShapeDtypeStruct(state.shape, bf16),
        in_specs=[pl.BlockSpec(memory_space=pltpu.SMEM)] + [VMEM] * 6,
        out_specs=VMEM,
        compiler_params=SMALL,
        name="update_atoms",
    )(counts, *on_chip(*near, state, gain[None, :], w_in, w_out))


def layer(positions, counts, feats, waves, wave_filter, mixing, gain, w_in, w_out):
    kw = waves.shape[1]
    share = kw // NZ
    own_waves = share // NYX
    atoms_all = feats.shape[0] * NZ * NYX * NC
    kwaves_all = kw * NC
    z = lax.axis_index("z")
    yx = lax.axis_index("y") * NX + lax.axis_index("x")
    swap = [(0, 1), (1, 0)]

    def partner(v):
        return lax.ppermute(v, "core", swap)

    def shift(v, d):
        return lax.ppermute(v, "z", [(i, (i + d) % NZ) for i in range(NZ)]) if d else v

    def exchange(v):
        return lax.all_to_all(v, ("y", "x"), 0, 0, tiled=True)

    block, mine, filt = pack(
        counts, z, z * NYX + yx, positions, feats, waves, wave_filter, share, own_waves
    )
    other = partner(mine)
    opposite = shift(block, HALF)
    ahead = shift(block, -2)
    behind = shift(block, 2)
    pair = jnp.concatenate([block, opposite], axis=0)
    near_behind = shift(pair, 1)
    near_ahead = shift(pair, -1)
    early = [ahead, behind, opposite, block]
    early_layout = [(0, 0), (1, 0), (2, 0), (3, 0)]
    late = [near_behind, near_ahead]
    late_layout = [(0, 1), (1, 1), (1, 0), (0, 0)]
    ready_other, ready_mine, part_other, part_mine = early_factors(
        [other, mine], early, early_layout
    )
    sent, tile_other = factors(other, part_other, late, late_layout, bf16)
    arrived = partner(sent)
    kept, tile_mine = factors(mine, part_mine, late, late_layout, f32)
    summed = exchange((kept + arrived.astype(f32)).astype(bf16))
    spread = filter_mix(summed, filt, mixing, 1.0 / math.sqrt(atoms_all))
    filtered = exchange(spread)
    filtered_other = partner(filtered)
    ready = own_fields((ready_mine, tile_mine), filtered)
    to_ahead, to_behind, far, own, one_ahead, one_behind = fields(
        (ready_other, tile_other),
        filtered_other,
        ready,
        [
            ([(0, 0), (1, 0)], bf16),
            ([(0, 1), (1, 1)], bf16),
            ([(0, 2)], bf16),
            ([(0, 3)], f32),
            ([(1, 2)], f32),
            ([(1, 3)], f32),
        ],
    )
    from_behind = shift(to_ahead, 2)
    from_ahead = shift(to_behind, -2)
    opposite = shift(far, HALF)
    one_ahead = (one_ahead + from_behind[1:].astype(f32)).astype(bf16)
    one_behind = (one_behind + from_ahead[1:].astype(f32)).astype(bf16)
    near_behind = shift(one_ahead, 1)
    near_ahead = shift(one_behind, -1)
    scale = 1.0 / math.sqrt(kwaves_all)
    state = early_state([own, from_ahead, from_behind, opposite], feats, scale)
    return update(counts, (near_behind, near_ahead), state, gain, w_in, w_out, scale)


def solution(mesh):
    fine = Mesh(mesh.devices.reshape(NZ, NY, NX, NC), ("z", "y", "x", "core"))
    every = ("z", "y", "x", "core")
    return jax.shard_map(
        layer,
        mesh=fine,
        in_specs=(
            P(None, every),
            P(every),
            P(every, None),
            P(None, "core"),
            P("core", None),
            P(),
            P(),
            P(),
            P(),
        ),
        out_specs=P(every, None),
        check_vma=False,
    )
```
